32 devices in a mesh: dp: 8 (over z, core), mp: 4 (over y, x).
Axes of the slice: x: 2, y: 2, z: 4, core: 2. Of those that a mesh axis runs over, the one named last changes fastest.
Arguments:
- inputs: bfloat16 [1024, 32768], P('dp', 'mp'), may hold values from -6 to 6
- cotangent: bfloat16 [1024, 32768], P('dp', 'mp'), may hold values from -6 to 6
- first_weight: bfloat16 [128, 2, 256, 256], P('mp', None, 'dp'), may hold values from -0.25 to 0.25
- second_weight: bfloat16 [128, 2, 256, 256], P('mp', None, 'dp'), may hold values from -0.25 to 0.25
- orders: int32 [2, 256], replicated, may hold values from 0 to 255, each once within a row
Outputs:
- input_grad: bfloat16 [1024, 32768], P('dp', 'mp')
- first_grad: float32 [128, 2, 256, 256], P('mp', None, 'dp')
- second_grad: float32 [128, 2, 256, 256], P('mp', None, 'dp')
The draws below stay inside these ranges and needn't reach their ends.
Inputs may be any that keep to these rules, and one draw needn't show every extreme that they name: Each of the two rows of orders is a permutation of 0 to 255.
All inputs are finite; a program needn't handle non-finite values.
Results may differ from the reference program's by a relative error of at most 0.018.
Values may be sent and summed in bfloat16 or wider, within the bound.
A program may use at most 128 MiB of HBM per device.

```python
import math
import jax
import jax.numpy as jnp
import numpy as np
from jax import lax

H = 32768
B = 256
TOK_DEV = 128
TOKENS = 1024


def levels(rng, shape, shards, low, largest):
    loudness, own = 1.0, jax.random.fold_in(rng, 6)
    for dim, parts in shards:
        steps = jnp.exp(jax.random.uniform(jax.random.fold_in(own, dim), (parts,), jnp.float32, low / len(shards), largest / len(shards)))
        loudness = loudness * jnp.repeat(steps, shape[dim] // parts).reshape([-1 if axis == dim else 1 for axis in range(len(shape))])
    return loudness


def normal_values(key, shape, deviation, reach, pieces=(), held_as=jnp.bfloat16):
    array = deviation * jax.random.normal(key, shape, jnp.float32)
    if pieces:
        array = array * levels(key, shape, pieces, -0.22, 0.18)
    return jnp.clip(array, -reach, reach).astype(held_as)


def setup_inputs(seed: int = 0) -> dict:
    key_of = jax.random.split(jax.random.key(seed), 6)
    return {
        "inputs": normal_values(key_of[0], (TOKENS, H), 1.0, 6.0, ((0, 8), (1, 4))),
        "cotangent": normal_values(key_of[1], (TOKENS, H), 1.0, 6.0, ((0, 8), (1, 4))),
        "first_weight": normal_values(key_of[2], (H // B, 2, B, B), (2 * B) ** -0.5, 0.25, ((0, 4), (2, 8))),
        "second_weight": normal_values(key_of[3], (H // B, 2, B, B), (2 * B) ** -0.5, 0.25, ((0, 4), (2, 8))),
        "orders": jax.vmap(lambda own: jax.random.permutation(own, B))(jax.random.split(key_of[4], 2)).reshape((2, B)).astype(jnp.int32),
    }


def gelu_tanh(argument):
    return jax.nn.gelu(argument, approximate=True)

def rounded(argument):
    return lax.optimization_barrier(argument.astype(jnp.bfloat16)).astype(jnp.float32)

def inverse_order(order):
    length = order.shape[0]
    positions = jnp.arange(length, dtype=jnp.int32)
    matches = order[None, :] == positions[:, None]
    return lax.optimization_barrier(jnp.sum(jnp.where(matches, positions[None, :], 0), axis=1)).astype(jnp.int32)

def contract(left, right):
    return jnp.einsum('tnk,nkj->tnj', left, right)

def contract_back(left, right):
    return jnp.einsum('tnj,nkj->tnk', left, right)

def outer_sum(left, right):
    return jnp.einsum('tnk,tnj->nkj', left, right)

def reference(inputs, cotangent, first_weight, second_weight, orders):
    block_count = H // B
    block_index = np.arange(block_count)
    first_partner = (block_index + block_count // 2) % block_count
    quarter = block_count // 4
    second_partner = np.where(block_index // quarter % 2 == 0, block_index + quarter, block_index - quarter)
    order_first = orders[0]
    order_second = orders[1]
    inverse_first = inverse_order(order_first)
    inverse_second = inverse_order(order_second)
    first_float = first_weight.astype(jnp.float32)
    second_float = second_weight.astype(jnp.float32)
    grad_scale = 1.0 / math.sqrt(TOKENS)
    group_count = TOKENS // TOK_DEV
    group_inputs = inputs.reshape(group_count, TOK_DEV, block_count, B)
    group_cot = cotangent.reshape(group_count, TOK_DEV, block_count, B)

    def group_step(carry, group_pair):
        first_acc, second_acc = carry
        tokens_in = group_pair[0].astype(jnp.float32)
        tokens_cot = group_pair[1].astype(jnp.float32)
        partner_in = tokens_in[:, first_partner]
        pre_act = contract(tokens_in, first_float[:, 0]) + contract(partner_in[:, :, order_first], first_float[:, 1])
        saved_pre = rounded(pre_act)
        activated = rounded(gelu_tanh(pre_act))
        cross_two = rounded(contract_back(tokens_cot, second_float[:, 1])[:, second_partner][:, :, inverse_second])
        act_grad = contract_back(tokens_cot, second_float[:, 0]) + cross_two
        pullback = jax.vjp(gelu_tanh, saved_pre)[1]
        pre_grad = rounded(pullback(act_grad)[0])
        cross_one = rounded(contract_back(pre_grad, first_float[:, 1])[:, first_partner][:, :, inverse_first])
        input_grad = (contract_back(pre_grad, first_float[:, 0]) + cross_one).astype(jnp.bfloat16)
        first_part = jnp.stack([outer_sum(tokens_in, pre_grad), outer_sum(partner_in, pre_grad)[:, order_first, :]], axis=1)
        second_part = jnp.stack([outer_sum(activated, tokens_cot), outer_sum(activated[:, second_partner], tokens_cot)[:, order_second, :]], axis=1)
        first_acc = first_acc + rounded(first_part * grad_scale)
        second_acc = second_acc + rounded(second_part * grad_scale)
        return ((first_acc, second_acc), input_grad)
    zeros_grad = jnp.zeros((block_count, 2, B, B), jnp.float32)
    sums, grads_in = lax.scan(group_step, (zeros_grad, zeros_grad), (group_inputs, group_cot))
    input_grad = grads_in.reshape(TOKENS, H)
    return (input_grad, sums[0], sums[1])
```

```python
import functools
import math

import jax
import jax.numpy as jnp
from jax import lax
from jax.experimental import pallas as pl
from jax.experimental.pallas import tpu as pltpu
from jax.sharding import PartitionSpec as P

B = 256
MESH = pl.DeviceIdType.MESH
ANY = pl.BlockSpec(memory_space=pl.ANY)
NT = (((1,), (1,)), ((), ()))
TN = (((0,), (0,)), ((), ()))


class Plan:
    def __init__(self, dp, mp, local_blocks):
        self.dp, self.mp, self.nb = dp, mp, local_blocks
        self.low = mp // 4
        g = max(1, dp // 2)
        while local_blocks % (4 * g):
            g //= 2
        self.g, self.groups = g, dp // g
        self.nq = local_blocks // (4 * g)

    def here(self):
        d, m = lax.axis_index("dp"), lax.axis_index("mp")
        return d, d // self.g, d % self.g, m // self.low, m % self.low


def greet(plan, d, h, lo):
    barrier = pltpu.get_barrier_semaphore()
    others = 4 * plan.dp
    me = d * 4 + h
    for k in range(1, others):
        t = (me + k) % others
        pl.semaphore_signal(
            barrier, inc=1, device_id=(t // 4, (t % 4) * plan.low + lo), device_id_type=MESH
        )
    pl.semaphore_wait(barrier, others - 1)


def run(remote, local):
    for c in remote:
        c.start()
    for c in local:
        c.start()
    for c in local:
        c.wait()
    for c in remote:
        c.wait()


def bring(plan, x, c, w1, w2, xo, co, w1o, w2o, ts, tr, ws, wr, ls):
    d, gi, r, h, lo = plan.here()
    tok = x.shape[0]
    rows = w1.shape[2]
    wide = plan.nq * B
    greet(plan, d, h, lo)

    def tokens(a, src, dst, k):
        n = 4 * plan.g
        me = r * 4 + h
        t = (me + k) % n
        s = src.at[:, pl.ds(pl.multiple_of(t * wide, wide), wide)]
        e = dst.at[h, pl.ds(pl.multiple_of(r * tok, tok), tok)]
        if k == 0:
            return pltpu.make_async_copy(s, e, ls.at[a])
        return pltpu.make_async_remote_copy(
            s, e, ts.at[a, k], tr.at[a, k],
            device_id=(gi * plan.g + t // 4, (t % 4) * plan.low + lo), device_id_type=MESH,
        )

    def weights(a, src, dst, k):
        n = 4 * plan.dp
        me = d * 4 + h
        t = (me + k) % n
        td, th = t // 4, t % 4
        o = (td % plan.g) * 4 + th
        s = src.at[pl.ds(o * plan.nq, plan.nq)]
        e = dst.at[h, :, :, pl.ds(pl.multiple_of(d * rows, rows), rows)]
        if k == 0:
            return pltpu.make_async_copy(s, e, ls.at[2 + a])
        return pltpu.make_async_remote_copy(
            s, e, ws.at[a, k], wr.at[a, k],
            device_id=(td, th * plan.low + lo), device_id_type=MESH,
        )

    remote = []
    for k in range(1, 4 * plan.dp):
        remote += [weights(0, w1, w1o, k), weights(1, w2, w2o, k)]
        if k < 4 * plan.g:
            remote += [tokens(0, x, xo, k), tokens(1, c, co, k)]
    local = [tokens(0, x, xo, 0), tokens(1, c, co, 0), weights(0, w1, w1o, 0), weights(1, w2, w2o, 0)]
    run(remote, local)


def send_back(plan, ig, gf, gs, igo, gfo, gso, ts, tr, ws, wr, ls):
    d, gi, r, h, lo = plan.here()
    tok = igo.shape[0]
    rows = gfo.shape[3]
    wide = plan.nq * B
    greet(plan, d, h, lo)
    me_o = r * 4 + h

    def tokens(k):
        n = 4 * plan.g
        t = (me_o + k) % n
        s = ig.at[t % 4, pl.ds(pl.multiple_of((t // 4) * tok, tok), tok)]
        e = igo.at[:, pl.ds(pl.multiple_of(me_o * wide, wide), wide)]
        if k == 0:
            return pltpu.make_async_copy(s, e, ls.at[0])
        return pltpu.make_async_remote_copy(
            s, e, ts.at[k], tr.at[k],
            device_id=(gi * plan.g + t // 4, (t % 4) * plan.low + lo), device_id_type=MESH,
        )

    def grads(a, src, dst, k):
        n = 4 * plan.dp
        t = (d * 4 + h + k) % n
        td, th = t // 4, t % 4
        s = src.at[th, :, :, pl.ds(pl.multiple_of(td * rows, rows), rows)]
        e = dst.at[gi, pl.ds(me_o * plan.nq, plan.nq)]
        if k == 0:
            return pltpu.make_async_copy(s, e, ls.at[1 + a])
        return pltpu.make_async_remote_copy(
            s, e, ws.at[a, k], wr.at[a, k],
            device_id=(td, th * plan.low + lo), device_id_type=MESH,
        )

    remote = []
    for k in range(1, 4 * plan.dp):
        remote += [grads(0, gf, gfo, k), grads(1, gs, gso, k)]
        if k < 4 * plan.g:
            remote += [tokens(k)]
    local = [tokens(0), grads(0, gf, gfo, 0), grads(1, gs, gso, 0)]
    run(remote, local)


def dot(left, right, dims=(((1,), (0,)), ((), ()))):
    return lax.dot_general(left, right, dims, preferred_element_type=jnp.float32)


def factors(scale, order, x, c, w1, w2, ig, gf, gs, w1p, w2p, act, pre):
    bf = jnp.bfloat16
    place = lax.broadcasted_iota(jnp.int32, (B, B), 0)
    spread_one = (place == order[0:1, :]).astype(jnp.float32).astype(bf)
    spread_two = (place == order[1:2, :]).astype(jnp.float32).astype(bf)
    root = math.sqrt(2.0 / math.pi)
    for h in range(4):
        w1p[h] = dot(spread_one, w1[h, 0, 1]).astype(bf)
        w2p[h] = dot(spread_two, w2[h, 0, 1]).astype(bf)
    for h in range(4):
        p, q = h ^ 2, h ^ 1
        v = dot(x[h], w1[h, 0, 0]) + dot(x[p], w1p[h])
        up = dot(c[h], w2[h, 0, 0], NT) + dot(c[q], w2p[q], NT)
        v2 = v * v
        t = jnp.tanh(root * v * (1.0 + 0.044715 * v2))
        half = 0.5 + 0.5 * t
        act[h] = (v * half).astype(bf)
        slope = half + (0.5 * root) * v * (1.0 - t * t) * (1.0 + (3 * 0.044715) * v2)
        pre[h] = (up * slope).astype(bf)
    for h in range(4):
        p, q = h ^ 2, h ^ 1
        ig[h] = (dot(pre[h], w1[h, 0, 0], NT) + dot(pre[p], w1p[p], NT)).astype(bf)
        gf[h, 0, 0] = (dot(x[h], pre[h], TN) * scale).astype(bf)
        cross = (dot(x[p], pre[h], TN) * scale).astype(bf)
        gf[h, 0, 1] = dot(spread_one, cross, TN).astype(bf)
        gs[h, 0, 0] = (dot(act[h], c[h], TN) * scale).astype(bf)
        cross = (dot(act[q], c[h], TN) * scale).astype(bf)
        gs[h, 0, 1] = dot(spread_two, cross, TN).astype(bf)


def shards(plan, inputs, cotangent, first_weight, second_weight, orders):
    tok, width = inputs.shape
    rows = first_weight.shape[2]
    bf = jnp.bfloat16
    all_tok = plan.g * tok
    nq = plan.nq
    scale = 1.0 / math.sqrt(tok * plan.dp)
    toks = jax.ShapeDtypeStruct((4, all_tok, nq * B), bf)
    mats = jax.ShapeDtypeStruct((4, nq, 2, B, B), bf)
    dma = pltpu.SemaphoreType.DMA
    n_t, n_w = 4 * plan.g, 4 * plan.dp
    x, c, w1, w2 = pl.pallas_call(
        functools.partial(bring, plan),
        out_shape=(toks, toks, mats, mats),
        in_specs=[ANY] * 4,
        out_specs=(ANY,) * 4,
        scratch_shapes=[dma((2, n_t)), dma((2, n_t)), dma((2, n_w)), dma((2, n_w)), dma((4,))],
        compiler_params=pltpu.CompilerParams(collective_id=0, has_side_effects=True),
        name="bring",
    )(inputs, cotangent, first_weight, second_weight)
    tok_spec = pl.BlockSpec((4, all_tok, B), lambda i: (0, 0, i))
    mat_spec = pl.BlockSpec((4, 1, 2, B, B), lambda i: (0, i, 0, 0, 0))
    ig, gf, gs = pl.pallas_call(
        functools.partial(factors, scale),
        out_shape=(toks, mats, mats),
        grid=(nq,),
        in_specs=[pl.BlockSpec((2, B), lambda i: (0, 0)), tok_spec, tok_spec, mat_spec, mat_spec],
        out_specs=(tok_spec, mat_spec, mat_spec),
        scratch_shapes=[
            pltpu.VMEM((4, B, B), bf),
            pltpu.VMEM((4, B, B), bf),
            pltpu.VMEM((4, all_tok, B), bf),
            pltpu.VMEM((4, all_tok, B), bf),
        ],
        compiler_params=pltpu.CompilerParams(vmem_limit_bytes=56 * 2**20),
        name="factors",
    )(orders, x, c, w1, w2)
    part = jax.ShapeDtypeStruct((plan.groups, plan.nb, 2, rows, B), bf)
    input_grad, first, second = pl.pallas_call(
        functools.partial(send_back, plan),
        out_shape=(jax.ShapeDtypeStruct((tok, width), bf), part, part),
        in_specs=[ANY] * 3,
        out_specs=(ANY,) * 3,
        scratch_shapes=[dma((n_t,)), dma((n_t,)), dma((2, n_w)), dma((2, n_w)), dma((3,))],
        compiler_params=pltpu.CompilerParams(collective_id=1, has_side_effects=True),
        name="send_back",
    )(ig, gf, gs)
    total = lambda parts: jnp.sum(parts.astype(jnp.float32), axis=0)
    return input_grad, total(first), total(second)


def solution(mesh):
    in_specs = (
        P("dp", "mp"),
        P("dp", "mp"),
        P("mp", None, "dp", None),
        P("mp", None, "dp", None),
        P(),
    )
    out_specs = (P("dp", "mp"), P("mp", None, "dp", None), P("mp", None, "dp", None))

    def body(inputs, *rest):
        plan = Plan(mesh.shape["dp"], mesh.shape["mp"], inputs.shape[1] // B)
        return shards(plan, inputs, *rest)

    return jax.shard_map(body, mesh=mesh, in_specs=in_specs, out_specs=out_specs, check_vma=False)
```

```python
import functools
import math

import jax
import jax.numpy as jnp
from jax import lax
from jax.experimental import pallas as pl
from jax.experimental.pallas import tpu as pltpu
from jax.sharding import PartitionSpec as P

B = 256
MESH = pl.DeviceIdType.MESH
ANY = pl.BlockSpec(memory_space=pl.ANY)
NT = (((1,), (1,)), ((), ()))
TN = (((0,), (0,)), ((), ()))


class Plan:
    def __init__(self, dp, mp, local_blocks):
        self.dp, self.mp, self.nb = dp, mp, local_blocks
        self.low = mp // 4
        g = max(1, dp // 2)
        while local_blocks % (4 * g):
            g //= 2
        self.g, self.groups = g, dp // g
        self.nq = local_blocks // (4 * g)

    def here(self):
        d, m = lax.axis_index("dp"), lax.axis_index("mp")
        return d, d // self.g, d % self.g, m // self.low, m % self.low


def greet(plan, d, h, lo):
    barrier = pltpu.get_barrier_semaphore()
    others = 4 * plan.dp
    me = d * 4 + h
    for k in range(1, others):
        t = (me + k) % others
        pl.semaphore_signal(
            barrier, inc=1, device_id=(t // 4, (t % 4) * plan.low + lo), device_id_type=MESH
        )
    pl.semaphore_wait(barrier, others - 1)


def sweep(first, last, body):
    lax.fori_loop(first, last, lambda k, _: (body(k), None)[1], None)


def whole(plan, scale, order, x, c, w1, w2, igo, gfo, gso, xb, cb, w1b, w2b, ig, gf, gs, w1p, w2p, act, pre,
          ts, tr, ws, wr, ls, os, orr, gsem, gr, ol):
    d, gi, r, h, lo = plan.here()
    tok, rows, nq = x.shape[0], w1.shape[2], plan.nq
    n_t, n_w = 4 * plan.g, 4 * plan.dp
    me_o, me_w = r * 4 + h, d * 4 + h
    greet(plan, d, h, lo)

    def peer_of_group(t):
        return (gi * plan.g + t // 4, (t % 4) * plan.low + lo)

    def peer_of_all(t):
        return (t // 4, (t % 4) * plan.low + lo)

    def tokens_in(i, a, k):
        t = (me_o + k) % n_t
        src, dst = ((x, xb), (c, cb))[a]
        s = src.at[:, pl.ds(pl.multiple_of((t * nq + i) * B, B), B)]
        e = dst.at[i, h, pl.ds(pl.multiple_of(r * tok, tok), tok)]
        if isinstance(k, int) and k == 0:
            return pltpu.make_async_copy(s, e, ls.at[i, a])
        return pltpu.make_async_remote_copy(
            s, e, ts.at[i, a, k], tr.at[i, a, k], device_id=peer_of_group(t), device_id_type=MESH
        )

    def weights_in(i, a, k):
        t = (me_w + k) % n_w
        src, dst = ((w1, w1b), (w2, w2b))[a]
        o = ((t // 4) % plan.g) * 4 + t % 4
        s = src.at[o * nq + i]
        e = dst.at[i, h, :, pl.ds(pl.multiple_of(d * rows, rows), rows)]
        if isinstance(k, int) and k == 0:
            return pltpu.make_async_copy(s, e, ls.at[i, 2 + a])
        return pltpu.make_async_remote_copy(
            s, e, ws.at[i, a, k], wr.at[i, a, k], device_id=peer_of_all(t), device_id_type=MESH
        )

    def tokens_out(i, k):
        t = (me_o + k) % n_t
        s = ig.at[i, t % 4, pl.ds(pl.multiple_of((t // 4) * tok, tok), tok)]
        e = igo.at[:, pl.ds(pl.multiple_of((me_o * nq + i) * B, B), B)]
        if isinstance(k, int) and k == 0:
            return pltpu.make_async_copy(s, e, ol.at[i, 0])
        return pltpu.make_async_remote_copy(
            s, e, os.at[i, k], orr.at[i, k], device_id=peer_of_group(t), device_id_type=MESH
        )

    def grads_out(i, a, k):
        t = (me_w + k) % n_w
        src, dst = ((gf, gfo), (gs, gso))[a]
        s = src.at[i, t % 4, :, pl.ds(pl.multiple_of((t // 4) * rows, rows), rows)]
        e = dst.at[gi, me_o * nq + i]
        if isinstance(k, int) and k == 0:
            return pltpu.make_async_copy(s, e, ol.at[i, 1 + a])
        return pltpu.make_async_remote_copy(
            s, e, gsem.at[i, a, k], gr.at[i, a, k], device_id=peer_of_all(t), device_id_type=MESH
        )

    def all_in(i, act_on):
        def near(k):
            for a in (0, 1):
                act_on(weights_in(i, a, k))
                act_on(tokens_in(i, a, k))

        def far(k):
            for a in (0, 1):
                act_on(weights_in(i, a, k))

        sweep(1, n_t, near)
        sweep(n_t, n_w, far)

    def all_out(i, act_on):
        def near(k):
            act_on(grads_out(i, 0, k))
            act_on(grads_out(i, 1, k))
            act_on(tokens_out(i, k))

        def far(k):
            act_on(grads_out(i, 0, k))
            act_on(grads_out(i, 1, k))

        sweep(1, n_t, near)
        sweep(n_t, n_w, far)

    def own_in(i):
        return [f(i, a, 0) for f in (tokens_in, weights_in) for a in (0, 1)]

    def own_out(i):
        return [tokens_out(i, 0), grads_out(i, 0, 0), grads_out(i, 1, 0)]

    for i in range(nq):
        all_in(i, lambda copy: copy.start())
        for copy in own_in(i):
            copy.start()
    for i in range(nq):
        for copy in own_in(i):
            copy.wait()
        all_in(i, lambda copy: copy.wait_recv())
        factors(scale, order, xb.at[i], cb.at[i], w1b.at[i], w2b.at[i], ig.at[i], gf.at[i], gs.at[i], w1p, w2p, act, pre)
        all_out(i, lambda copy: copy.start())
        for copy in own_out(i):
            copy.start()
    for i in range(nq):
        all_in(i, lambda copy: copy.wait_send())
        for copy in own_out(i):
            copy.wait()
        all_out(i, lambda copy: copy.wait())


def dot(left, right, dims=(((1,), (0,)), ((), ()))):
    return lax.dot_general(left, right, dims, preferred_element_type=jnp.float32)


def factors(scale, order, x, c, w1, w2, ig, gf, gs, w1p, w2p, act, pre):
    bf = jnp.bfloat16
    place = lax.broadcasted_iota(jnp.int32, (B, B), 0)
    spread_one = (place == order[0:1, :]).astype(jnp.float32).astype(bf)
    spread_two = (place == order[1:2, :]).astype(jnp.float32).astype(bf)
    root = math.sqrt(2.0 / math.pi)
    for h in range(4):
        w1p[h] = dot(spread_one, w1[h, 1]).astype(bf)
        w2p[h] = dot(spread_two, w2[h, 1]).astype(bf)
    for h in range(4):
        p, q = h ^ 2, h ^ 1
        v = dot(x[h], w1[h, 0]) + dot(x[p], w1p[h])
        up = dot(c[h], w2[h, 0], NT) + dot(c[q], w2p[q], NT)
        v2 = v * v
        t = jnp.tanh(root * v * (1.0 + 0.044715 * v2))
        half = 0.5 + 0.5 * t
        act[h] = (v * half).astype(bf)
        slope = half + (0.5 * root) * v * (1.0 - t * t) * (1.0 + (3 * 0.044715) * v2)
        pre[h] = (up * slope).astype(bf)
    for h in range(4):
        p, q = h ^ 2, h ^ 1
        ig[h] = (dot(pre[h], w1[h, 0], NT) + dot(pre[p], w1p[p], NT)).astype(bf)
        gf[h, 0] = (dot(x[h], pre[h], TN) * scale).astype(bf)
        cross = (dot(x[p], pre[h], TN) * scale).astype(bf)
        gf[h, 1] = dot(spread_one, cross, TN).astype(bf)
        gs[h, 0] = (dot(act[h], c[h], TN) * scale).astype(bf)
        cross = (dot(act[q], c[h], TN) * scale).astype(bf)
        gs[h, 1] = dot(spread_two, cross, TN).astype(bf)


def shards(plan, inputs, cotangent, first_weight, second_weight, orders):
    tok, width = inputs.shape
    rows = first_weight.shape[2]
    bf = jnp.bfloat16
    all_tok = plan.g * tok
    nq = plan.nq
    scale = 1.0 / math.sqrt(tok * plan.dp)
    dma = pltpu.SemaphoreType.DMA
    n_t, n_w = 4 * plan.g, 4 * plan.dp
    toks = pltpu.VMEM((nq, 4, all_tok, B), bf)
    mats = pltpu.VMEM((nq, 4, 2, B, B), bf)
    part = jax.ShapeDtypeStruct((plan.groups, plan.nb, 2, rows, B), bf)
    input_grad, first, second = pl.pallas_call(
        functools.partial(whole, plan, scale),
        out_shape=(jax.ShapeDtypeStruct((tok, width), bf), part, part),
        in_specs=[pl.BlockSpec(memory_space=pltpu.VMEM)] + [ANY] * 4,
        out_specs=(ANY,) * 3,
        scratch_shapes=[toks, toks, mats, mats, toks, mats, mats]
        + [pltpu.VMEM((4, B, B), bf)] * 2
        + [pltpu.VMEM((4, all_tok, B), bf)] * 2
        + [dma((nq, 2, n_t)), dma((nq, 2, n_t)), dma((nq, 2, n_w)), dma((nq, 2, n_w)), dma((nq, 4))]
        + [dma((nq, n_t)), dma((nq, n_t)), dma((nq, 2, n_w)), dma((nq, 2, n_w)), dma((nq, 3))],
        compiler_params=pltpu.CompilerParams(
            collective_id=0, has_side_effects=True, vmem_limit_bytes=56 * 2**20
        ),
        name="whole",
    )(orders, inputs, cotangent, first_weight, second_weight)
    total = lambda parts: jnp.sum(parts.astype(jnp.float32), axis=0)
    return input_grad, total(first), total(second)


def solution(mesh):
    in_specs = (
        P("dp", "mp"),
        P("dp", "mp"),
        P("mp", None, "dp", None),
        P("mp", None, "dp", None),
        P(),
    )
    out_specs = (P("dp", "mp"), P("mp", None, "dp", None), P("mp", None, "dp", None))

    def body(inputs, *rest):
        plan = Plan(mesh.shape["dp"], mesh.shape["mp"], inputs.shape[1] // B)
        return shards(plan, inputs, *rest)

    return jax.shard_map(body, mesh=mesh, in_specs=in_specs, out_specs=out_specs, check_vma=False)
```

```python
import functools
import math

import jax
import jax.numpy as jnp
from jax import lax
from jax.experimental import pallas as pl
from jax.experimental.pallas import tpu as pltpu
from jax.sharding import PartitionSpec as P

B = 256
MESH = pl.DeviceIdType.MESH
ANY = pl.BlockSpec(memory_space=pl.ANY)
NT = (((1,), (1,)), ((), ()))
TN = (((0,), (0,)), ((), ()))


class Plan:
    def __init__(self, dp, mp, local_blocks):
        self.dp, self.mp, self.nb = dp, mp, local_blocks
        self.low = mp // 4
        g = max(1, dp // 2)
        while local_blocks % (4 * g):
            g //= 2
        self.g, self.groups = g, dp // g
        self.nq = local_blocks // (4 * g)

    def here(self):
        d, m = lax.axis_index("dp"), lax.axis_index("mp")
        return d, d // self.g, d % self.g, m // self.low, m % self.low


def greet(plan, d, h, lo):
    barrier = pltpu.get_barrier_semaphore()
    others = 4 * plan.dp
    me = d * 4 + h
    for k in range(1, others):
        t = (me + k) % others
        pl.semaphore_signal(
            barrier, inc=1, device_id=(t // 4, (t % 4) * plan.low + lo), device_id_type=MESH
        )
    pl.semaphore_wait(barrier, others - 1)


def sweep(first, last, body):
    lax.fori_loop(first, last, lambda k, _: (body(k), None)[1], None)


def whole(plan, scale, order, x, c, w1, w2, igo, gfo, gso, xb, cb, w1b, w2b, ig, gf, gs, w1p, w2p, act, pre,
          ts, tr, ws, wr, ls, os, orr, gsem, gr, ol):
    d, gi, r, h, lo = plan.here()
    tok, rows, nq = x.shape[0], w1.shape[2], plan.nq
    n_t, n_w = 4 * plan.g, 4 * plan.dp
    me_o, me_w = r * 4 + h, d * 4 + h
    greet(plan, d, h, lo)

    def peer_of_group(t):
        return (gi * plan.g + t // 4, (t % 4) * plan.low + lo)

    def peer_of_all(t):
        return (t // 4, (t % 4) * plan.low + lo)

    def tokens_in(i, a, k):
        t = (me_o + 5 * k) % n_t
        src, dst = ((x, xb), (c, cb))[a]
        s = src.at[:, pl.ds(pl.multiple_of((t * nq + i) * B, B), B)]
        e = dst.at[i, h, pl.ds(pl.multiple_of(r * tok, tok), tok)]
        if isinstance(k, int) and k == 0:
            return pltpu.make_async_copy(s, e, ls.at[i, a])
        return pltpu.make_async_remote_copy(
            s, e, ts.at[i, a, k], tr.at[i, a, k], device_id=peer_of_group(t), device_id_type=MESH
        )

    def weights_in(i, a, k):
        t = (me_w + 11 * k) % n_w
        src, dst = ((w1, w1b), (w2, w2b))[a]
        o = ((t // 4) % plan.g) * 4 + t % 4
        s = src.at[o * nq + i]
        e = dst.at[i, h, :, pl.ds(pl.multiple_of(d * rows, rows), rows)]
        if isinstance(k, int) and k == 0:
            return pltpu.make_async_copy(s, e, ls.at[i, 2 + a])
        return pltpu.make_async_remote_copy(
            s, e, ws.at[i, a, k], wr.at[i, a, k], device_id=peer_of_all(t), device_id_type=MESH
        )

    def tokens_out(i, k):
        t = (me_o + 5 * k) % n_t
        s = ig.at[i, t % 4, pl.ds(pl.multiple_of((t // 4) * tok, tok), tok)]
        e = igo.at[:, pl.ds(pl.multiple_of((me_o * nq + i) * B, B), B)]
        if isinstance(k, int) and k == 0:
            return pltpu.make_async_copy(s, e, ol.at[i, 0])
        return pltpu.make_async_remote_copy(
            s, e, os.at[i, k], orr.at[i, k], device_id=peer_of_group(t), device_id_type=MESH
        )

    def grads_out(i, a, k):
        t = (me_w + 11 * k) % n_w
        src, dst = ((gf, gfo), (gs, gso))[a]
        s = src.at[i, t % 4, :, pl.ds(pl.multiple_of((t // 4) * rows, rows), rows)]
        e = dst.at[gi, me_o * nq + i]
        if isinstance(k, int) and k == 0:
            return pltpu.make_async_copy(s, e, ol.at[i, 1 + a])
        return pltpu.make_async_remote_copy(
            s, e, gsem.at[i, a, k], gr.at[i, a, k], device_id=peer_of_all(t), device_id_type=MESH
        )

    def all_in(i, act_on):
        def some_weights(k, first):
            for j in range(first, plan.groups):
                for a in (0, 1):
                    act_on(weights_in(i, a, plan.groups * k + j))

        def both(k):
            act_on(tokens_in(i, 0, k))
            some_weights(k, 0)
            act_on(tokens_in(i, 1, k))

        some_weights(0, 1)
        sweep(1, n_t, both)

    def all_out(i, act_on):
        def some_grads(k, first):
            for j in range(first, plan.groups):
                for a in (0, 1):
                    act_on(grads_out(i, a, plan.groups * k + j))

        def both(k):
            act_on(tokens_out(i, k))
            some_grads(k, 0)

        some_grads(0, 1)
        sweep(1, n_t, both)

    def own_in(i):
        return [f(i, a, 0) for f in (tokens_in, weights_in) for a in (0, 1)]

    def own_out(i):
        return [tokens_out(i, 0), grads_out(i, 0, 0), grads_out(i, 1, 0)]

    for i in range(nq):
        all_in(i, lambda copy: copy.start())
        for copy in own_in(i):
            copy.start()
    for i in range(nq):
        for copy in own_in(i):
            copy.wait()
        all_in(i, lambda copy: copy.wait_recv())
        factors(scale, order, xb.at[i], cb.at[i], w1b.at[i], w2b.at[i], ig.at[i], gf.at[i], gs.at[i], w1p, w2p, act, pre)
        all_out(i, lambda copy: copy.start())
        for copy in own_out(i):
            copy.start()
    for i in range(nq):
        all_in(i, lambda copy: copy.wait_send())
        for copy in own_out(i):
            copy.wait()
        all_out(i, lambda copy: copy.wait())


def dot(left, right, dims=(((1,), (0,)), ((), ()))):
    return lax.dot_general(left, right, dims, preferred_element_type=jnp.float32)


def factors(scale, order, x, c, w1, w2, ig, gf, gs, w1p, w2p, act, pre):
    bf = jnp.bfloat16
    place = lax.broadcasted_iota(jnp.int32, (B, B), 0)
    spread_one = (place == order[0:1, :]).astype(jnp.float32).astype(bf)
    spread_two = (place == order[1:2, :]).astype(jnp.float32).astype(bf)
    root = math.sqrt(2.0 / math.pi)
    for h in range(4):
        w1p[h] = dot(spread_one, w1[h, 1]).astype(bf)
        w2p[h] = dot(spread_two, w2[h, 1]).astype(bf)
    for h in range(4):
        p, q = h ^ 2, h ^ 1
        v = dot(x[h], w1[h, 0]) + dot(x[p], w1p[h])
        up = dot(c[h], w2[h, 0], NT) + dot(c[q], w2p[q], NT)
        v2 = v * v
        t = jnp.tanh(root * v * (1.0 + 0.044715 * v2))
        half = 0.5 + 0.5 * t
        act[h] = (v * half).astype(bf)
        slope = half + (0.5 * root) * v * (1.0 - t * t) * (1.0 + (3 * 0.044715) * v2)
        pre[h] = (up * slope).astype(bf)
    for h in range(4):
        p, q = h ^ 2, h ^ 1
        ig[h] = (dot(pre[h], w1[h, 0], NT) + dot(pre[p], w1p[p], NT)).astype(bf)
        gf[h, 0] = (dot(x[h], pre[h], TN) * scale).astype(bf)
        cross = (dot(x[p], pre[h], TN) * scale).astype(bf)
        gf[h, 1] = dot(spread_one, cross, TN).astype(bf)
        gs[h, 0] = (dot(act[h], c[h], TN) * scale).astype(bf)
        cross = (dot(act[q], c[h], TN) * scale).astype(bf)
        gs[h, 1] = dot(spread_two, cross, TN).astype(bf)


def shards(plan, inputs, cotangent, first_weight, second_weight, orders):
    tok, width = inputs.shape
    rows = first_weight.shape[2]
    bf = jnp.bfloat16
    all_tok = plan.g * tok
    nq = plan.nq
    scale = 1.0 / math.sqrt(tok * plan.dp)
    dma = pltpu.SemaphoreType.DMA
    n_t, n_w = 4 * plan.g, 4 * plan.dp
    toks = pltpu.VMEM((nq, 4, all_tok, B), bf)
    mats = pltpu.VMEM((nq, 4, 2, B, B), bf)
    part = jax.ShapeDtypeStruct((plan.groups, plan.nb, 2, rows, B), bf)
    input_grad, first, second = pl.pallas_call(
        functools.partial(whole, plan, scale),
        out_shape=(jax.ShapeDtypeStruct((tok, width), bf), part, part),
        in_specs=[pl.BlockSpec(memory_space=pltpu.VMEM)] + [ANY] * 4,
        out_specs=(ANY,) * 3,
        scratch_shapes=[toks, toks, mats, mats, toks, mats, mats]
        + [pltpu.VMEM((4, B, B), bf)] * 2
        + [pltpu.VMEM((4, all_tok, B), bf)] * 2
        + [dma((nq, 2, n_t)), dma((nq, 2, n_t)), dma((nq, 2, n_w)), dma((nq, 2, n_w)), dma((nq, 4))]
        + [dma((nq, n_t)), dma((nq, n_t)), dma((nq, 2, n_w)), dma((nq, 2, n_w)), dma((nq, 3))],
        compiler_params=pltpu.CompilerParams(
            collective_id=0, has_side_effects=True, vmem_limit_bytes=56 * 2**20
        ),
        name="whole",
    )(orders, inputs, cotangent, first_weight, second_weight)
    total = lambda parts: jnp.sum(parts.astype(jnp.float32), axis=0)
    return input_grad, total(first), total(second)


def solution(mesh):
    in_specs = (
        P("dp", "mp"),
        P("dp", "mp"),
        P("mp", None, "dp", None),
        P("mp", None, "dp", None),
        P(),
    )
    out_specs = (P("dp", "mp"), P("mp", None, "dp", None), P("mp", None, "dp", None))

    def body(inputs, *rest):
        plan = Plan(mesh.shape["dp"], mesh.shape["mp"], inputs.shape[1] // B)
        return shards(plan, inputs, *rest)

    return jax.shard_map(body, mesh=mesh, in_specs=in_specs, out_specs=out_specs, check_vma=False)
```

```python
import functools
import math

import jax
import jax.numpy as jnp
from jax import lax
from jax.experimental import pallas as pl
from jax.experimental.pallas import tpu as pltpu
from jax.sharding import PartitionSpec as P

B = 256
MESH = pl.DeviceIdType.MESH
ANY = pl.BlockSpec(memory_space=pl.ANY)
NT = (((1,), (1,)), ((), ()))
TN = (((0,), (0,)), ((), ()))


class Plan:
    def __init__(self, dp, mp, local_blocks):
        self.dp, self.mp, self.nb = dp, mp, local_blocks
        self.low = mp // 4
        g = max(1, dp // 2)
        while local_blocks % (4 * g):
            g //= 2
        self.g, self.groups = g, dp // g
        self.nq = local_blocks // (4 * g)

    def here(self):
        d, m = lax.axis_index("dp"), lax.axis_index("mp")
        return d, d // self.g, d % self.g, m // self.low, m % self.low


def greet(plan, d, h, lo):
    barrier = pltpu.get_barrier_semaphore()
    others = 4 * plan.dp
    me = d * 4 + h
    for k in range(1, others):
        t = (me + k) % others
        pl.semaphore_signal(
            barrier, inc=1, device_id=(t // 4, (t % 4) * plan.low + lo), device_id_type=MESH
        )
    pl.semaphore_wait(barrier, others - 1)


def sweep(first, last, body):
    lax.fori_loop(first, last, lambda k, _: (body(k), None)[1], None)


def whole(plan, scale, order, x, c, w1, w2, igo, gfo, gso, xb, cb, w1b, w2b, ig, gf, gs, w1p, w2p, act, pre,
          ts, tr, ws, wr, ls, os, orr, gsem, gr, ol):
    d, gi, r, h, lo = plan.here()
    tok, rows, nq = x.shape[0], w1.shape[2], plan.nq
    n_t, n_w = 4 * plan.g, 4 * plan.dp
    me_o, me_w = r * 4 + h, d * 4 + h
    greet(plan, d, h, lo)

    def peer_of_group(t):
        return (gi * plan.g + t // 4, (t % 4) * plan.low + lo)

    def peer_of_all(t):
        return (t // 4, (t % 4) * plan.low + lo)

    def tokens_in(i, a, k):
        t = (me_o + 5 * k) % n_t
        src, dst = ((x, xb), (c, cb))[a]
        s = src.at[:, pl.ds(pl.multiple_of((t * nq + i) * B, B), B)]
        e = dst.at[i, h, pl.ds(pl.multiple_of(r * tok, tok), tok)]
        if isinstance(k, int) and k == 0:
            return pltpu.make_async_copy(s, e, ls.at[i, a])
        return pltpu.make_async_remote_copy(
            s, e, ts.at[i, a, k], tr.at[i, a, k], device_id=peer_of_group(t), device_id_type=MESH
        )

    def weights_in(i, a, k):
        t = (me_w + 11 * k) % n_w
        src, dst = ((w1, w1b), (w2, w2b))[a]
        o = ((t // 4) % plan.g) * 4 + t % 4
        s = src.at[o * nq + i]
        e = dst.at[i, h, :, pl.ds(pl.multiple_of(d * rows, rows), rows)]
        if isinstance(k, int) and k == 0:
            return pltpu.make_async_copy(s, e, ls.at[i, 2 + a])
        return pltpu.make_async_remote_copy(
            s, e, ws.at[i, a, k], wr.at[i, a, k], device_id=peer_of_all(t), device_id_type=MESH
        )

    def tokens_out(i, k):
        t = (me_o + 5 * k) % n_t
        s = ig.at[i, t % 4, pl.ds(pl.multiple_of((t // 4) * tok, tok), tok)]
        e = igo.at[:, pl.ds(pl.multiple_of((me_o * nq + i) * B, B), B)]
        if isinstance(k, int) and k == 0:
            return pltpu.make_async_copy(s, e, ol.at[i, 0])
        return pltpu.make_async_remote_copy(
            s, e, os.at[i, k], orr.at[i, k], device_id=peer_of_group(t), device_id_type=MESH
        )

    def grads_out(i, a, k):
        t = (me_w + 11 * k) % n_w
        src, dst = ((gf, gfo), (gs, gso))[a]
        s = src.at[i, t % 4, :, pl.ds(pl.multiple_of((t // 4) * rows, rows), rows)]
        e = dst.at[gi, me_o * nq + i]
        if isinstance(k, int) and k == 0:
            return pltpu.make_async_copy(s, e, ol.at[i, 1 + a])
        return pltpu.make_async_remote_copy(
            s, e, gsem.at[i, a, k], gr.at[i, a, k], device_id=peer_of_all(t), device_id_type=MESH
        )

    def all_in(i, act_on):
        def some_weights(k, first):
            for j in range(first, plan.groups):
                for a in (0, 1):
                    act_on(weights_in(i, a, plan.groups * k + j))

        def both(k):
            act_on(tokens_in(i, 0, k))
            some_weights(k, 0)
            act_on(tokens_in(i, 1, k))

        some_weights(0, 1)
        sweep(1, n_t, both)

    def all_out(i, act_on):
        def some_grads(k, first):
            for j in range(first, plan.groups):
                for a in (0, 1):
                    act_on(grads_out(i, a, plan.groups * k + j))

        def both(k):
            act_on(tokens_out(i, k))
            some_grads(k, 0)

        some_grads(0, 1)
        sweep(1, n_t, both)

    def own_in(i):
        return [f(i, a, 0) for f in (tokens_in, weights_in) for a in (0, 1)]

    def own_out(i):
        return [tokens_out(i, 0), grads_out(i, 0, 0), grads_out(i, 1, 0)]

    for i in range(nq):
        all_in(i, lambda copy: copy.start())
        for copy in own_in(i):
            copy.start()
    for i in range(nq):
        for copy in own_in(i):
            copy.wait()
        all_in(i, lambda copy: copy.wait_recv())
        factors(scale, order, xb.at[i], cb.at[i], w1b.at[i], w2b.at[i], ig.at[i], gf.at[i], gs.at[i], w1p, w2p, act, pre)
        all_out(i, lambda copy: copy.start())
        for copy in own_out(i):
            copy.start()
    for i in range(nq):
        all_in(i, lambda copy: copy.wait_send())
        for copy in own_out(i):
            copy.wait()
        all_out(i, lambda copy: copy.wait())


def dot(left, right, dims=(((1,), (0,)), ((), ()))):
    return lax.dot_general(left, right, dims, preferred_element_type=jnp.float32)


def factors(scale, order, x, c, w1, w2, ig, gf, gs, w1p, w2p, act, pre):
    bf = jnp.bfloat16
    place = lax.broadcasted_iota(jnp.int32, (B, B), 0)
    spread_one = (place == order[0:1, :]).astype(jnp.float32).astype(bf)
    spread_two = (place == order[1:2, :]).astype(jnp.float32).astype(bf)
    root = math.sqrt(2.0 / math.pi)
    for h in range(4):
        w1p[h] = dot(spread_one, w1[h, 1]).astype(bf)
        w2p[h] = dot(spread_two, w2[h, 1]).astype(bf)
    for h in range(4):
        p, q = h ^ 2, h ^ 1
        v = dot(x[h], w1[h, 0]) + dot(x[p], w1p[h])
        up = dot(c[h], w2[h, 0], NT) + dot(c[q], w2p[q], NT)
        v2 = v * v
        t = jnp.tanh(root * v * (1.0 + 0.044715 * v2))
        half = 0.5 + 0.5 * t
        act[h] = (v * half).astype(bf)
        slope = half + (0.5 * root) * v * (1.0 - t * t) * (1.0 + (3 * 0.044715) * v2)
        pre[h] = (up * slope).astype(bf)
    for h in range(4):
        p, q = h ^ 2, h ^ 1
        ig[h] = (dot(pre[h], w1[h, 0], NT) + dot(pre[p], w1p[p], NT)).astype(bf)
        gf[h, 0] = (dot(x[h], pre[h], TN) * scale).astype(bf)
        cross = (dot(x[p], pre[h], TN) * scale).astype(bf)
        gf[h, 1] = dot(spread_one, cross, TN).astype(bf)
        gs[h, 0] = (dot(act[h], c[h], TN) * scale).astype(bf)
        cross = (dot(act[q], c[h], TN) * scale).astype(bf)
        gs[h, 1] = dot(spread_two, cross, TN).astype(bf)


def finish(one, two, grad, first, second, out):
    first[...] = jnp.sum(one[...].astype(jnp.float32), axis=0)
    second[...] = jnp.sum(two[...].astype(jnp.float32), axis=0)
    out[...] = grad[...]


def shards(plan, inputs, cotangent, first_weight, second_weight, orders):
    tok, width = inputs.shape
    rows = first_weight.shape[2]
    bf = jnp.bfloat16
    all_tok = plan.g * tok
    nq = plan.nq
    scale = 1.0 / math.sqrt(tok * plan.dp)
    dma = pltpu.SemaphoreType.DMA
    n_t, n_w = 4 * plan.g, 4 * plan.dp
    toks = pltpu.VMEM((nq, 4, all_tok, B), bf)
    mats = pltpu.VMEM((nq, 4, 2, B, B), bf)
    part = jax.ShapeDtypeStruct((plan.groups, plan.nb, 2, rows, B), bf)
    input_grad, first, second = pl.pallas_call(
        functools.partial(whole, plan, scale),
        out_shape=(jax.ShapeDtypeStruct((tok, width), bf), part, part),
        in_specs=[pl.BlockSpec(memory_space=pltpu.VMEM)] + [ANY] * 4,
        out_specs=(ANY,) * 3,
        scratch_shapes=[toks, toks, mats, mats, toks, mats, mats]
        + [pltpu.VMEM((4, B, B), bf)] * 2
        + [pltpu.VMEM((4, all_tok, B), bf)] * 2
        + [dma((nq, 2, n_t)), dma((nq, 2, n_t)), dma((nq, 2, n_w)), dma((nq, 2, n_w)), dma((nq, 4))]
        + [dma((nq, n_t)), dma((nq, n_t)), dma((nq, 2, n_w)), dma((nq, 2, n_w)), dma((nq, 3))],
        compiler_params=pltpu.CompilerParams(
            collective_id=0, has_side_effects=True, vmem_limit_bytes=56 * 2**20
        ),
        name="whole",
    )(orders, inputs, cotangent, first_weight, second_weight)
    steps = math.gcd(plan.nb, tok // 16, 8)
    each = plan.nb // steps
    part_spec = pl.BlockSpec((plan.groups, each, 2, rows, B), lambda i: (0, i, 0, 0, 0))
    sum_spec = pl.BlockSpec((each, 2, rows, B), lambda i: (i, 0, 0, 0))
    grad_spec = pl.BlockSpec((tok // steps, width), lambda i: (i, 0))
    summed = jax.ShapeDtypeStruct((plan.nb, 2, rows, B), jnp.float32)
    first, second, input_grad = pl.pallas_call(
        finish,
        grid=(steps,),
        out_shape=(summed, summed, jax.ShapeDtypeStruct((tok, width), bf)),
        in_specs=[part_spec, part_spec, grad_spec],
        out_specs=(sum_spec, sum_spec, grad_spec),
        compiler_params=pltpu.CompilerParams(vmem_limit_bytes=56 * 2**20),
        name="finish",
    )(first, second, input_grad)
    return input_grad, first, second


def solution(mesh):
    in_specs = (
        P("dp", "mp"),
        P("dp", "mp"),
        P("mp", None, "dp", None),
        P("mp", None, "dp", None),
        P(),
    )
    out_specs = (P("dp", "mp"), P("mp", None, "dp", None), P("mp", None, "dp", None))

    def body(inputs, *rest):
        plan = Plan(mesh.shape["dp"], mesh.shape["mp"], inputs.shape[1] // B)
        return shards(plan, inputs, *rest)

    return jax.shard_map(body, mesh=mesh, in_specs=in_specs, out_specs=out_specs, check_vma=False)
```
